512 devices in a mesh: slab: 32 (over y, x, core), cross: 16 (over z).
Axes of the slice: x: 4, y: 4, z: 16, core: 2. Of those that a mesh axis runs over, the one named last changes fastest.
Arguments:
- pore_mask: int32 [128, 256, 128], P('slab', 'cross'), may hold values from 0 to 1, as said below
- phase_labels: int32 [128, 256, 128], P('slab', 'cross'), may hold values 0 or 1
- velocity: float32 [3, 128, 256, 128], P(None, 'slab', 'cross'), may hold values from -0.3 to 0.3
Outputs:
- phase_field: float32 [128, 256, 128], P('slab', 'cross')
- populations: float32 [19, 128, 256, 128], P(None, 'slab', 'cross')
The draws below stay inside these ranges and needn't reach their ends.
Inputs may be any that keep to these rules, and one draw needn't show every extreme that they name: `pore_mask`: 1 marks a pore voxel. `phase_labels`: 1 marks the first fluid.
All inputs are finite; a program needn't handle non-finite values. No bound on the sum of `phase_labels` on one device may be relied on, other than what follows from the above.
Results may differ from the reference program's by a relative error of at most 0.0003.
Values sent between devices are 32-bit elements; how exact they have to be, the bound alone decides.
No kernel may reach another device: no remote copies, remote signals or barrier semaphores. Data moves between devices by JAX's collectives and lax.ppermute only.
A program may use at most 64 MiB of HBM per device.

```python
import jax
import jax.numpy as jnp

STEPS = 4
NX = 128
NY = 256
NZ = 128


def draw_pore_mask(key, part):
    seeds = jax.random.randint(jax.random.fold_in(key, 7), (NX, NY, NZ), 0, 8, dtype=jnp.int32)
    total = jnp.zeros((NX, NY, NZ), jnp.int32)
    for step_x in (-1, 0, 1):
        for step_y in (-1, 0, 1):
            for step_z in (-1, 0, 1):
                total = total + jnp.roll(seeds, (step_x, step_y, step_z), axis=(0, 1, 2))
    return jnp.where(total >= 101, 1, 0).astype(jnp.int32)


def plant(array, rng, smallest, largest):
    extent = array.shape
    place = [jax.random.randint(jax.random.fold_in(rng, axis), (), 0, extent[axis]) for axis in range(len(extent))]
    array = array.at[tuple(place)].set(smallest)
    longest = extent.index(max(extent))
    place[longest] = (place[longest] + 1) % extent[longest]
    return array.at[tuple(place)].set(largest)


def block_scale(own_key, shape, pieces, smallest, high):
    level = 1.0
    for position, shards_of in pieces:
        heights = jax.random.uniform(jax.random.fold_in(jax.random.fold_in(own_key, 6), position), (shards_of,), jnp.float32, smallest / len(pieces), high / len(pieces))
        level = level * jnp.repeat(jnp.exp(heights), shape[position] // shards_of).reshape((-1,) + (1,) * (len(shape) - 1 - position))
    return level


def noise(key, dims, deviation, bound, pieces=(), kind=jnp.bfloat16):
    values = jax.random.normal(key, dims, jnp.float32) * deviation
    if len(pieces) > 0:
        values = block_scale(key, dims, pieces, -0.22, 0.18) * values
    return jnp.clip(values, min=-bound, max=bound).astype(kind)


def setup_inputs(seed: int = 0) -> dict:
    splits = jax.random.split(jax.random.key(seed), 4)
    return {
        "pore_mask": draw_pore_mask(jax.random.fold_in(splits[3], 71), 0),
        "phase_labels": plant((jax.random.randint(splits[1], (NX, NY, NZ), 0, 2) < 1).astype(jnp.int32), jax.random.fold_in(splits[1], 1), 0, 1),
        "velocity": noise(splits[2], (3, NX, NY, NZ), 0.05, 0.3, ((1, 32), (2, 16)), jnp.float32),
    }


lattice_dirs = [(0, 0, 0), (1, 0, 0), (-1, 0, 0), (0, 1, 0), (0, -1, 0), (0, 0, 1), (0, 0, -1), (1, 1, 0), (-1, -1, 0), (1, -1, 0), (-1, 1, 0), (1, 0, 1), (-1, 0, -1), (1, 0, -1), (-1, 0, 1), (0, 1, 1), (0, -1, -1), (0, 1, -1), (0, -1, 1)]
lattice_weights = [1.0 / 3.0] + [1.0 / 18.0] * 6 + [1.0 / 36.0] * 12
tension_offsets = [-1.0 / 3.0] + [1.0 / 18.0] * 6 + [1.0 / 36.0] * 12
phase_weights = [0.25] + [0.125] * 6
relax_red = 1.0
relax_blue = 0.7
tension = 0.1
segregation = 0.7
driving = 0.001

def opposite(member):
    if member == 0:
        return 0
    return member + 1 if member % 2 == 1 else member - 1

def project(heading, vectors):
    summed = jnp.zeros_like(vectors[0])
    for component in range(3):
        if heading[component] != 0:
            summed = summed + float(heading[component]) * vectors[component]
    return summed

def momentum_equilibrium(density, velocity):
    speed_sq = velocity[0] * velocity[0] + velocity[1] * velocity[1] + velocity[2] * velocity[2]
    result = []
    for member in range(19):
        flow_dot = project(lattice_dirs[member], velocity)
        result.append(lattice_weights[member] * density * (1.0 + 3.0 * flow_dot + 4.5 * flow_dot * flow_dot - 1.5 * speed_sq))
    return result

def phase_update(red_mass, blue_mass, velocity, normal):
    red_pops = []
    blue_pops = []
    if normal is not None:
        mixed = segregation * red_mass * blue_mass / (red_mass + blue_mass)
    for member in range(7):
        heading = lattice_dirs[member]
        flow_dot = project(heading, velocity)
        red_new = red_mass * (1.0 + 4.0 * flow_dot)
        blue_new = blue_mass * (1.0 + 4.0 * flow_dot)
        if normal is not None:
            bias = mixed * project(heading, normal)
            red_new = red_new + bias
            blue_new = blue_new - bias
        red_pops.append(phase_weights[member] * red_new)
        blue_pops.append(phase_weights[member] * blue_new)
    return (red_pops, blue_pops)

def moments(populations, red_pops, blue_pops):
    density = populations[0]
    for member in range(1, 19):
        density = density + populations[member]
    velocity = []
    for component in range(3):
        summed = jnp.zeros_like(density)
        for member in range(19):
            offset = lattice_dirs[member][component]
            if offset != 0:
                summed = summed + float(offset) * populations[member]
        velocity.append(summed / density)
    red_mass = red_pops[0]
    blue_mass = blue_pops[0]
    for member in range(1, 7):
        red_mass = red_mass + red_pops[member]
        blue_mass = blue_mass + blue_pops[member]
    colour = (red_mass - blue_mass) / (red_mass + blue_mass)
    return (density, velocity, red_mass, blue_mass, colour)

def colour_gradient(neighbour, template):
    gradient = [jnp.zeros_like(template), jnp.zeros_like(template), jnp.zeros_like(template)]
    for member in range(1, 19):
        heading = lattice_dirs[member]
        nearby = neighbour(heading)
        for component in range(3):
            if heading[component] != 0:
                gradient[component] = gradient[component] + 3.0 * lattice_weights[member] * heading[component] * nearby
    return gradient

def collide(populations, density, velocity, red_mass, blue_mass, colour, gradient):
    relax = 0.5 * (1.0 + colour) * relax_red + 0.5 * (1.0 - colour) * relax_blue
    omega = 1.0 / relax
    equilibrium = momentum_equilibrium(density, velocity)
    grad_sq = gradient[0] * gradient[0] + gradient[1] * gradient[1] + gradient[2] * gradient[2]
    length = jnp.maximum(jnp.sqrt(grad_sq), 0.5)
    normal = [gradient[0] / length, gradient[1] / length, gradient[2] / length]
    post = []
    for member in range(19):
        heading = lattice_dirs[member]
        along_grad = project(heading, gradient)
        tensile = tension * (lattice_weights[member] * along_grad * along_grad - tension_offsets[member] * grad_sq)
        forcing = 3.0 * lattice_weights[member] * driving * heading[0] * density
        post.append(populations[member] - omega * (populations[member] - equilibrium[member]) + tensile + forcing)
    red_post, blue_post = phase_update(red_mass, blue_mass, velocity, normal)
    return (post, red_post, blue_post)

def stream(post, prior, pore, count):
    result = []
    for member in range(count):
        heading = lattice_dirs[member]
        pulled = jnp.roll(post[member], heading, axis=(0, 1, 2))
        opened = jnp.roll(pore, heading, axis=(0, 1, 2))
        moved = jnp.where(opened > 0, pulled, post[opposite(member)])
        result.append(jnp.where(pore > 0, moved, prior[member]))
    return result

def reference(pore_mask, phase_labels, velocity):
    labels = phase_labels.astype(jnp.float32)
    start_vel = [velocity[0], velocity[1], velocity[2]]
    populations = momentum_equilibrium(jnp.ones_like(labels), start_vel)
    red_pops, blue_pops = phase_update(labels, 1.0 - labels, start_vel, None)
    for iteration in range(STEPS):
        density, flow, red_mass, blue_mass, colour = moments(populations, red_pops, blue_pops)
        tinted = jnp.where(pore_mask > 0, colour, 0.0)

        def neighbour(heading):
            return jnp.roll(tinted, (-heading[0], -heading[1], -heading[2]), axis=(0, 1, 2))
        gradient = colour_gradient(neighbour, tinted)
        post, red_post, blue_post = collide(populations, density, flow, red_mass, blue_mass, colour, gradient)
        populations = stream(post, populations, pore_mask, 19)
        red_pops = stream(red_post, red_pops, pore_mask, 7)
        blue_pops = stream(blue_post, blue_pops, pore_mask, 7)
    density, flow, red_mass, blue_mass, colour = moments(populations, red_pops, blue_pops)
    return (jnp.where(pore_mask > 0, colour, 0.0), jnp.stack(populations))
```

```python
import jax
import jax.numpy as jnp
from jax import lax
from jax.experimental import pallas as pl
from jax.experimental.pallas import tpu as pltpu
from jax.sharding import PartitionSpec as P

STEPS = 4
HALO = 2 * STEPS
PAD = 8

lattice_dirs = [
    (0, 0, 0),
    (1, 0, 0),
    (-1, 0, 0),
    (0, 1, 0),
    (0, -1, 0),
    (0, 0, 1),
    (0, 0, -1),
    (1, 1, 0),
    (-1, -1, 0),
    (1, -1, 0),
    (-1, 1, 0),
    (1, 0, 1),
    (-1, 0, -1),
    (1, 0, -1),
    (-1, 0, 1),
    (0, 1, 1),
    (0, -1, -1),
    (0, 1, -1),
    (0, -1, 1),
]
relax_red = 1.0
relax_blue = 0.7
tension = 0.1
segregation = 0.7
driving = 0.001
LANES = 128


def turn(value, amount):
    return pltpu.roll(value, amount % LANES, axis=1)


def gradient_of(tint, x, y):
    at = {(dx, dy): tint[x + dx, pl.ds(y + dy, 8), :] for dx in (-1, 0, 1) for dy in (-1, 0, 1)}
    along_x = {dy: at[1, dy] - at[-1, dy] for dy in (-1, 0, 1)}
    along_y = {dx: at[dx, 1] - at[dx, -1] for dx in (-1, 0, 1)}
    gx = (along_x[0] + along_x[0]) + (along_x[1] + along_x[-1]) + (turn(along_x[0], 1) + turn(along_x[0], -1))
    gy = (along_y[0] + along_y[0]) + (along_y[1] + along_y[-1]) + (turn(along_y[0], 1) + turn(along_y[0], -1))
    mixed = (at[0, 0] + at[0, 0]) + (at[1, 0] + at[-1, 0]) + (at[0, 1] + at[0, -1])
    gz = turn(mixed, -1) - turn(mixed, 1)
    twelfth = 1.0 / 12.0
    return (gx * twelfth, gy * twelfth, gz * twelfth), at[0, 0]


PAIRS = ((7, 0, 1, 1), (9, 0, 1, -1), (11, 0, 2, 1), (13, 0, 2, -1), (15, 1, 2, 1), (17, 1, 2, -1))


def collide_tile(pulled, density, flow, omega, mass, colour, gradient):
    ux, uy, uz = flow
    gx, gy, gz = gradient
    grad_sq = gx * gx + gy * gy + gz * gz
    part = tension / 36.0
    tensed = [part * g for g in gradient]
    if pulled is None:
        drift = [(3.0 / 36.0) * u for u in flow]
        curve = [(4.5 / 36.0) * u for u in flow]
        push = 3.0 * driving / 36.0
        level = 1.0 / 36.0
    else:
        level = omega * density * (1.0 / 36.0)
        triple = 3.0 * level
        drift = [triple * u for u in flow]
        curve = [1.5 * d for d in drift]
        push = (3.0 * driving / 36.0) * density
    square = [c * u + t * g for c, u, t, g in zip(curve, flow, tensed, gradient)]
    total = square[0] + square[1] + square[2]
    tense_sq = part * grad_sq
    even = level - total * (1.0 / 3.0) - (2.0 / 3.0) * tense_sq
    drift = [drift[0] + push, drift[1], drift[2]]
    twice_c = [curve[0] + curve[0], curve[1] + curve[1]]
    twice_t = [tensed[0] + tensed[0], tensed[1] + tensed[1]]
    cross = {
        (0, 1): twice_c[0] * uy + twice_t[0] * gy,
        (0, 2): twice_c[0] * uz + twice_t[0] * gz,
        (1, 2): twice_c[1] * uz + twice_t[1] * gz,
    }
    base = [even + s for s in square]
    rest = 12.0 * level - 4.0 * total + 16.0 * tense_sq
    post = [None] * 19
    keep = None if pulled is None else 1.0 - omega

    def put(member, symmetric, skew):
        if pulled is None:
            post[member] = symmetric + skew
            post[member + 1] = symmetric - skew
        else:
            post[member] = keep * pulled[member] + (symmetric + skew)
            post[member + 1] = keep * pulled[member + 1] + (symmetric - skew)

    post[0] = rest if pulled is None else keep * pulled[0] + rest
    for axis in range(3):
        put(1 + 2 * axis, base[axis] + base[axis], drift[axis] + drift[axis])
    for a, b, first, second in ((0, 1, 7, 9), (0, 2, 11, 13), (1, 2, 15, 17)):
        plane = base[a] + square[b]
        put(first, plane + cross[a, b], drift[a] + drift[b])
        put(second, plane - cross[a, b], drift[a] - drift[b])

    shrink = jnp.minimum(lax.rsqrt(grad_sq), 2.0)
    if mass is None:
        eighth = 0.125
        sway = [0.5 * u for u in flow]
    else:
        eighth = 0.125 * mass
        half = 0.5 * mass
        sway = [half * u for u in flow]
    tinted = eighth * colour
    sharpen = (0.5 * segregation) * (eighth - tinted * colour) * shrink
    fluxes = []
    for axis in range(3):
        slope = sway[axis] * colour + sharpen * gradient[axis]
        fluxes += [eighth + sway[axis], eighth - sway[axis], tinted + slope, tinted - slope]
    return post, fluxes


def kernel(par_ref, e_ref, a_ref, b_ref, s_ref, phase_ref, out_ref, vel, tint, mass, open_, star, flux):
    own_x, own_y = phase_ref.shape[0], phase_ref.shape[1]
    rows, cols = own_x + 2 * HALO, own_y + 2 * HALO
    for ref, origin, start in (
        (e_ref, 0, HALO),
        (a_ref, 0, par_ref[0]),
        (b_ref, 0, par_ref[1]),
        (s_ref, 0, par_ref[2]),
        (s_ref, own_x, par_ref[3]),
    ):
        for r in range(own_x):
            for y in range(0, cols, 8):
                colour = ref[0, origin + r, pl.ds(y, 8), :]
                tint[start + r, pl.ds(PAD + y, 8), :] = colour
                pore = jnp.where(colour != 0.0, 1.0, 0.0)
                open_[0, start + r, pl.ds(PAD + y, 8), :] = pore
                open_[1, start + r, pl.ds(PAD + y, 8), :] = turn(pore, 1)
                open_[2, start + r, pl.ds(PAD + y, 8), :] = turn(pore, -1)
                for c in range(3):
                    vel[c, start + r, pl.ds(y, 8), :] = ref[1 + c, origin + r, pl.ds(y, 8), :]

    def spread(low, high, groups, body):
        def row(x, carry):
            for y in groups:
                body(x, y)
            return carry

        lax.fori_loop(low, high, row, 0)

    def pull(ref, lead, member, x, y):
        cx, cy, cz = lattice_dirs[member]
        value = ref[lead, x - cx, pl.ds(PAD + y - cy, 8), :]
        return turn(value, cz) if cz else value

    def is_open(member, x, y):
        cx, cy, cz = lattice_dirs[member]
        return open_[cz % 3, x - cx, pl.ds(PAD + y - cy, 8), :] > 0.0

    def write(target, x, y, post, fluxes):
        for member in range(19):
            star[target, member, x, pl.ds(PAD + y, 8), :] = post[member]
        for k in range(12):
            flux[k, x, pl.ds(PAD + y, 8), :] = fluxes[k]

    def first(x, y):
        gradient, colour = gradient_of(tint, x, PAD + y)
        flow = [vel[c, x, pl.ds(y, 8), :] for c in range(3)]
        post, fluxes = collide_tile(None, None, flow, None, None, colour, gradient)
        write(0, x, y, post, fluxes)
        mass[x, pl.ds(PAD + y, 8), :] = jnp.ones_like(colour)

    groups_of = {1: range(0, cols, 8), 2: range(0, cols, 8), 3: range(4, cols - 4, 8), 4: range(4, cols - 4, 8)}
    spread(1, rows - 1, groups_of[1], first)

    def masses(x, y):
        amount = 0.25 * mass[x, pl.ds(PAD + y, 8), :]
        tinted = amount * tint[x, pl.ds(PAD + y, 8), :]
        for member in range(1, 7):
            axis, sign = divmod(member - 1, 2)
            back = 1 - sign
            free = is_open(member, x, y)
            for k in range(2):
                moved = jnp.where(
                    free,
                    pull(flux, 4 * axis + 2 * k + sign, member, x, y),
                    flux[4 * axis + 2 * k + back, x, pl.ds(PAD + y, 8), :],
                )
                if k == 0:
                    amount = amount + moved
                else:
                    tinted = tinted + moved
        pore = open_[0, x, pl.ds(PAD + y, 8), :] > 0.0
        return amount, jnp.where(pore, tinted / amount, 0.0), pore

    def pulled_of(source, x, y):
        values = [star[source, 0, x, pl.ds(PAD + y, 8), :]]
        for member in range(1, 19):
            other = member + 1 if member % 2 == 1 else member - 1
            values.append(
                jnp.where(
                    is_open(member, x, y),
                    pull(star.at[source], member, member, x, y),
                    star[source, other, x, pl.ds(PAD + y, 8), :],
                )
            )
        return values

    for step in range(2, STEPS + 1):
        source = (step - 2) % 2

        def phases(x, y):
            amount, colour, _ = masses(x, y)
            mass[x, pl.ds(PAD + y, 8), :] = amount
            tint[x, pl.ds(PAD + y, 8), :] = colour

        def later(x, y, source=source):
            pulled = pulled_of(source, x, y)
            gradient, colour = gradient_of(tint, x, PAD + y)
            summed = {m: pulled[m] + pulled[m + 1] for m in range(1, 19, 2)}
            gap = {m: pulled[m] - pulled[m + 1] for m in range(1, 19, 2)}
            density = pulled[0] + (
                ((summed[1] + summed[3]) + (summed[5] + summed[7]))
                + ((summed[9] + summed[11]) + (summed[13] + summed[15]))
                + summed[17]
            )
            jx = gap[1] + ((gap[7] + gap[9]) + (gap[11] + gap[13]))
            jy = gap[3] + ((gap[7] - gap[9]) + (gap[15] + gap[17]))
            jz = gap[5] + ((gap[11] - gap[13]) + (gap[15] - gap[17]))
            lighten = 1.0 / density
            flow = [jx * lighten, jy * lighten, jz * lighten]
            omega = 1.0 / (0.5 * (relax_red + relax_blue) + (0.5 * (relax_red - relax_blue)) * colour)
            post, fluxes = collide_tile(
                pulled, density, flow, omega, mass[x, pl.ds(PAD + y, 8), :], colour, gradient
            )
            write(1 - source, x, y, post, fluxes)

        spread(2 * step - 2, rows - 2 * step + 2, groups_of[step], phases)
        spread(2 * step - 1, rows - 2 * step + 1, groups_of[step], later)

    last = (STEPS - 1) % 2

    def final(x, y):
        _, colour, pore = masses(x, y)
        phase_ref[x - HALO, pl.ds(y - HALO, 8), :] = colour
        values = pulled_of(last, x, y)
        flow = [vel[c, x, pl.ds(y, 8), :] for c in range(3)]
        speed = flow[0] * flow[0] + flow[1] * flow[1] + flow[2] * flow[2]
        for member in range(19):
            weight = 1.0 / 3.0 if member == 0 else 1.0 / 18.0 if member < 7 else 1.0 / 36.0
            dot = sum(float(c) * u for c, u in zip(lattice_dirs[member], flow) if c != 0)
            start = weight * (1.0 + 3.0 * dot + 4.5 * dot * dot - 1.5 * speed)
            out_ref[member, x - HALO, pl.ds(y - HALO, 8), :] = jnp.where(pore, values[member], start)

    spread(HALO, HALO + own_x, range(HALO, HALO + own_y, 8), final)


def advance(places, own, inner, outer, partner):
    own_x, cols = own.shape[1], own.shape[2]
    own_y = cols - 2 * HALO
    rows = own_x + 2 * HALO
    wide = cols + 2 * PAD
    vmem = pl.BlockSpec(memory_space=pltpu.VMEM)
    return pl.pallas_call(
        kernel,
        out_shape=(
            jax.ShapeDtypeStruct((own_x, own_y, LANES), jnp.float32),
            jax.ShapeDtypeStruct((19, own_x, own_y, LANES), jnp.float32),
        ),
        in_specs=[pl.BlockSpec(memory_space=pltpu.SMEM)] + [vmem] * 4,
        out_specs=(vmem, vmem),
        scratch_shapes=[
            pltpu.VMEM((3, rows, cols, LANES), jnp.float32),
            pltpu.VMEM((rows, wide, LANES), jnp.float32),
            pltpu.VMEM((rows, wide, LANES), jnp.float32),
            pltpu.VMEM((3, rows, wide, LANES), jnp.float32),
            pltpu.VMEM((2, 19, rows, wide, LANES), jnp.float32),
            pltpu.VMEM((12, rows, wide, LANES), jnp.float32),
        ],
        compiler_params=pltpu.CompilerParams(vmem_limit_bytes=48 * 1024 * 1024),
    )(places, own, inner, outer, partner)


def exchange(array, axis, width, pairing):
    devices = lax.axis_size(axis)
    groups = devices // width
    moves = []
    for i in range(devices):
        group, place = divmod(i, width)
        step = 1 if group % 2 == pairing else -1
        moves.append((i, (group + step) % groups * width + place))
    return lax.ppermute(array, axis, moves)


def shards(pore_mask, phase_labels, velocity):
    own_x, own_y = pore_mask.shape[0], pore_mask.shape[1]
    slab, cross = lax.axis_index("slab"), lax.axis_index("cross")
    core, chip = slab % 2, slab // 2 % 2
    colour = jnp.where(pore_mask > 0, 2.0 * phase_labels.astype(jnp.float32) - 1.0, 0.0)
    block = jnp.concatenate([colour[None], velocity])
    low, high = block[:, :, :HALO], block[:, :, own_y - HALO :]
    odd = cross % 2 == 1
    near = exchange(jnp.where(odd, low, high), "cross", 1, 0)
    far = exchange(jnp.where(odd, high, low), "cross", 1, 1)
    own = jnp.concatenate([jnp.where(odd, near, far), block, jnp.where(odd, far, near)], axis=2)
    outer = exchange(own, "slab", 2, 1)
    inner = exchange(own, "slab", 2, 0)
    passed = jnp.where(core == chip, inner, outer)
    partner = exchange(jnp.concatenate([own, passed], axis=1), "slab", 1, 0)
    inner_at = jnp.where(chip == 0, HALO + 2 * own_x, 0)
    partner_at = jnp.where(core == 0, HALO + own_x, HALO - own_x)
    places = jnp.stack([inner_at, HALO + 2 * own_x - inner_at, partner_at, 2 * HALO - partner_at])
    return advance(places.astype(jnp.int32), own, inner, outer, partner)


def solution(mesh):
    in_specs = (P("slab", "cross", None), P("slab", "cross", None), P(None, "slab", "cross", None))
    out_specs = (P("slab", "cross", None), P(None, "slab", "cross", None))
    return jax.shard_map(shards, mesh=mesh, in_specs=in_specs, out_specs=out_specs, check_vma=False)
```

```python
import jax
import jax.numpy as jnp
from jax import lax
from jax.experimental import pallas as pl
from jax.experimental.pallas import tpu as pltpu
from jax.sharding import PartitionSpec as P


STEPS = 4
HALO = 2 * STEPS
PAD = 8

lattice_dirs = [
    (0, 0, 0),
    (1, 0, 0),
    (-1, 0, 0),
    (0, 1, 0),
    (0, -1, 0),
    (0, 0, 1),
    (0, 0, -1),
    (1, 1, 0),
    (-1, -1, 0),
    (1, -1, 0),
    (-1, 1, 0),
    (1, 0, 1),
    (-1, 0, -1),
    (1, 0, -1),
    (-1, 0, 1),
    (0, 1, 1),
    (0, -1, -1),
    (0, 1, -1),
    (0, -1, 1),
]
relax_red = 1.0
relax_blue = 0.7
tension = 0.1
segregation = 0.7
driving = 0.001
LANES = 128


def turn(value, amount):
    return pltpu.roll(value, amount % LANES, axis=1)


def gradient_of(tint, x, y):
    at = {(dx, dy): tint[x + dx, pl.ds(y + dy, 8), :] for dx in (-1, 0, 1) for dy in (-1, 0, 1)}
    along_x = {dy: at[1, dy] - at[-1, dy] for dy in (-1, 0, 1)}
    along_y = {dx: at[dx, 1] - at[dx, -1] for dx in (-1, 0, 1)}
    gx = (along_x[0] + along_x[0]) + (along_x[1] + along_x[-1]) + (turn(along_x[0], 1) + turn(along_x[0], -1))
    gy = (along_y[0] + along_y[0]) + (along_y[1] + along_y[-1]) + (turn(along_y[0], 1) + turn(along_y[0], -1))
    mixed = (at[0, 0] + at[0, 0]) + (at[1, 0] + at[-1, 0]) + (at[0, 1] + at[0, -1])
    gz = turn(mixed, -1) - turn(mixed, 1)
    twelfth = 1.0 / 12.0
    return (gx * twelfth, gy * twelfth, gz * twelfth), at[0, 0]


def collide_tile(pulled, density, flow, omega, mass, colour, gradient):
    _, uy, uz = flow
    gx, gy, gz = gradient
    grad_sq = gx * gx + gy * gy + gz * gz
    part = tension / 36.0
    tensed = [part * g for g in gradient]
    if pulled is None:
        drift = [(3.0 / 36.0) * u for u in flow]
        curve = [(4.5 / 36.0) * u for u in flow]
        push = 3.0 * driving / 36.0
        level = 1.0 / 36.0
    else:
        level = omega * density * (1.0 / 36.0)
        triple = 3.0 * level
        drift = [triple * u for u in flow]
        curve = [1.5 * d for d in drift]
        push = (3.0 * driving / 36.0) * density
    square = [c * u + t * g for c, u, t, g in zip(curve, flow, tensed, gradient)]
    total = square[0] + square[1] + square[2]
    tense_sq = part * grad_sq
    even = level - total * (1.0 / 3.0) - (2.0 / 3.0) * tense_sq
    drift = [drift[0] + push, drift[1], drift[2]]
    twice_c = [curve[0] + curve[0], curve[1] + curve[1]]
    twice_t = [tensed[0] + tensed[0], tensed[1] + tensed[1]]
    cross = {
        (0, 1): twice_c[0] * uy + twice_t[0] * gy,
        (0, 2): twice_c[0] * uz + twice_t[0] * gz,
        (1, 2): twice_c[1] * uz + twice_t[1] * gz,
    }
    base = [even + s for s in square]
    rest = 12.0 * level - 4.0 * total + 16.0 * tense_sq
    post = [None] * 19
    keep = None if pulled is None else 1.0 - omega

    def put(member, symmetric, skew):
        if pulled is None:
            post[member] = symmetric + skew
            post[member + 1] = symmetric - skew
        else:
            post[member] = keep * pulled[member] + (symmetric + skew)
            post[member + 1] = keep * pulled[member + 1] + (symmetric - skew)

    post[0] = rest if pulled is None else keep * pulled[0] + rest
    for axis in range(3):
        put(1 + 2 * axis, base[axis] + base[axis], drift[axis] + drift[axis])
    for a, b, first, second in ((0, 1, 7, 9), (0, 2, 11, 13), (1, 2, 15, 17)):
        plane = base[a] + square[b]
        put(first, plane + cross[a, b], drift[a] + drift[b])
        put(second, plane - cross[a, b], drift[a] - drift[b])

    shrink = jnp.minimum(lax.rsqrt(grad_sq), 2.0)
    if mass is None:
        eighth = 0.125
        sway = [0.5 * u for u in flow]
    else:
        eighth = 0.125 * mass
        half = 0.5 * mass
        sway = [half * u for u in flow]
    tinted = eighth * colour
    sharpen = (0.5 * segregation) * (eighth - tinted * colour) * shrink
    fluxes = []
    for axis in range(3):
        slope = sway[axis] * colour + sharpen * gradient[axis]
        fluxes += [eighth + sway[axis], eighth - sway[axis], tinted + slope, tinted - slope]
    return post, fluxes


def kernel(par_ref, e_ref, a_ref, b_ref, s_ref, phase_ref, out_ref, vel, open_, flux, *doubled):
    tints, amounts, stars = doubled[0:2], doubled[2:4], doubled[4:6]
    own_x, own_y = phase_ref.shape[0], phase_ref.shape[1]
    rows, cols = own_x + 2 * HALO, own_y + 2 * HALO
    for ref, origin, start in (
        (e_ref, 0, HALO),
        (a_ref, 0, par_ref[0]),
        (b_ref, 0, par_ref[1]),
        (s_ref, 0, par_ref[2]),
        (s_ref, own_x, par_ref[3]),
    ):
        for r in range(own_x):
            for y in range(0, cols, 8):
                colour = ref[0, origin + r, pl.ds(y, 8), :]
                tints[0][start + r, pl.ds(PAD + y, 8), :] = colour
                pore = jnp.where(colour != 0.0, 1.0, 0.0)
                open_[0, start + r, pl.ds(PAD + y, 8), :] = pore
                open_[1, start + r, pl.ds(PAD + y, 8), :] = turn(pore, 1)
                open_[2, start + r, pl.ds(PAD + y, 8), :] = turn(pore, -1)
                for c in range(3):
                    vel[c, start + r, pl.ds(y, 8), :] = ref[1 + c, origin + r, pl.ds(y, 8), :]

    def spread(low, high, groups, body, tiles=None):
        count = len(groups)
        tiles = tiles or count

        def some(i, carry):
            if tiles >= count:
                for x in range(tiles // count):
                    for y in groups:
                        body(low + i * (tiles // count) + x, y)
            else:
                parts = count // tiles
                x, part = low + i // parts, i % parts
                for k in range(tiles):
                    body(x, groups[0] + 8 * (part * tiles + k))
            return carry

        lax.fori_loop(0, (high - low) * count // tiles, some, 0)

    def pull(ref, lead, member, x, y):
        cx, cy, cz = lattice_dirs[member]
        value = ref[lead, x - cx, pl.ds(PAD + y - cy, 8), :]
        return turn(value, cz) if cz else value

    def is_open(member, x, y):
        cx, cy, cz = lattice_dirs[member]
        return open_[cz % 3, x - cx, pl.ds(PAD + y - cy, 8), :] > 0.0

    def write(target, x, y, post, fluxes):
        for member in range(19):
            stars[target][member, x, pl.ds(PAD + y, 8), :] = post[member]
        for k in range(12):
            flux[k, x, pl.ds(PAD + y, 8), :] = fluxes[k]

    def first(x, y):
        gradient, colour = gradient_of(tints[0], x, PAD + y)
        flow = [vel[c, x, pl.ds(y, 8), :] for c in range(3)]
        post, fluxes = collide_tile(None, None, flow, None, None, colour, gradient)
        write(0, x, y, post, fluxes)
        amounts[0][x, pl.ds(PAD + y, 8), :] = jnp.ones_like(colour)

    groups_of = {1: range(0, cols, 8), 2: range(0, cols, 8), 3: range(4, cols - 4, 8), 4: range(4, cols - 4, 8)}
    spread(1, rows - 1, groups_of[1], first, 4)

    def masses(source, x, y):
        amount = 0.25 * amounts[source][x, pl.ds(PAD + y, 8), :]
        tinted = amount * tints[source][x, pl.ds(PAD + y, 8), :]
        for member in range(1, 7):
            axis, sign = divmod(member - 1, 2)
            back = 1 - sign
            free = is_open(member, x, y)
            for k in range(2):
                moved = jnp.where(
                    free,
                    pull(flux, 4 * axis + 2 * k + sign, member, x, y),
                    flux[4 * axis + 2 * k + back, x, pl.ds(PAD + y, 8), :],
                )
                if k == 0:
                    amount = amount + moved
                else:
                    tinted = tinted + moved
        pore = open_[0, x, pl.ds(PAD + y, 8), :] > 0.0
        return amount, jnp.where(pore, tinted / amount, 0.0), pore

    def pulled_of(source, x, y):
        values = [stars[source][0, x, pl.ds(PAD + y, 8), :]]
        for member in range(1, 19):
            other = member + 1 if member % 2 == 1 else member - 1
            values.append(
                jnp.where(
                    is_open(member, x, y),
                    pull(stars[source], member, member, x, y),
                    stars[source][other, x, pl.ds(PAD + y, 8), :],
                )
            )
        return values

    for step in range(2, STEPS + 1):
        source = (step - 2) % 2

        def phases(x, y, source=source):
            amount, colour, _ = masses(source, x, y)
            amounts[1 - source][x, pl.ds(PAD + y, 8), :] = amount
            tints[1 - source][x, pl.ds(PAD + y, 8), :] = colour

        def later(x, y, source=source):
            pulled = pulled_of(source, x, y)
            gradient, colour = gradient_of(tints[1 - source], x, PAD + y)
            summed = {m: pulled[m] + pulled[m + 1] for m in range(1, 19, 2)}
            gap = {m: pulled[m] - pulled[m + 1] for m in range(1, 19, 2)}
            density = pulled[0] + (
                ((summed[1] + summed[3]) + (summed[5] + summed[7]))
                + ((summed[9] + summed[11]) + (summed[13] + summed[15]))
                + summed[17]
            )
            jx = gap[1] + ((gap[7] + gap[9]) + (gap[11] + gap[13]))
            jy = gap[3] + ((gap[7] - gap[9]) + (gap[15] + gap[17]))
            jz = gap[5] + ((gap[11] - gap[13]) + (gap[15] - gap[17]))
            lighten = 1.0 / density
            flow = [jx * lighten, jy * lighten, jz * lighten]
            omega = 1.0 / (0.5 * (relax_red + relax_blue) + (0.5 * (relax_red - relax_blue)) * colour)
            amount = amounts[1 - source][x, pl.ds(PAD + y, 8), :]
            post, fluxes = collide_tile(pulled, density, flow, omega, amount, colour, gradient)
            write(1 - source, x, y, post, fluxes)

        spread(2 * step - 2, rows - 2 * step + 2, groups_of[step], phases, 16 if step == 2 else 12)
        spread(2 * step - 1, rows - 2 * step + 1, groups_of[step], later, len(groups_of[step]))

    last = (STEPS - 1) % 2

    def final(x, y):
        _, colour, pore = masses(last, x, y)
        phase_ref[x - HALO, pl.ds(y - HALO, 8), :] = colour
        values = pulled_of(last, x, y)
        flow = [vel[c, x, pl.ds(y, 8), :] for c in range(3)]
        speed = flow[0] * flow[0] + flow[1] * flow[1] + flow[2] * flow[2]
        for member in range(19):
            weight = 1.0 / 3.0 if member == 0 else 1.0 / 18.0 if member < 7 else 1.0 / 36.0
            dot = sum(float(c) * u for c, u in zip(lattice_dirs[member], flow) if c != 0)
            start = weight * (1.0 + 3.0 * dot + 4.5 * dot * dot - 1.5 * speed)
            out_ref[member, x - HALO, pl.ds(y - HALO, 8), :] = jnp.where(pore, values[member], start)

    spread(HALO, HALO + own_x, range(HALO, HALO + own_y, 8), final)


def advance(places, own, inner, outer, partner):
    own_x, cols = own.shape[1], own.shape[2]
    own_y = cols - 2 * HALO
    rows = own_x + 2 * HALO
    wide = cols + 2 * PAD
    vmem = pl.BlockSpec(memory_space=pltpu.VMEM)
    return pl.pallas_call(
        kernel,
        out_shape=(
            jax.ShapeDtypeStruct((own_x, own_y, LANES), jnp.float32),
            jax.ShapeDtypeStruct((19, own_x, own_y, LANES), jnp.float32),
        ),
        in_specs=[pl.BlockSpec(memory_space=pltpu.SMEM)] + [vmem] * 4,
        out_specs=(vmem, vmem),
        scratch_shapes=[
            pltpu.VMEM((3, rows, cols, LANES), jnp.float32),
            pltpu.VMEM((3, rows, wide, LANES), jnp.float32),
            pltpu.VMEM((12, rows, wide, LANES), jnp.float32),
        ]
        + [pltpu.VMEM((rows, wide, LANES), jnp.float32)] * 4
        + [pltpu.VMEM((19, rows, wide, LANES), jnp.float32)] * 2,
        compiler_params=pltpu.CompilerParams(vmem_limit_bytes=48 * 1024 * 1024),
    )(places, own, inner, outer, partner)


def exchange(array, axis, width, pairing):
    devices = lax.axis_size(axis)
    groups = devices // width
    moves = []
    for i in range(devices):
        group, place = divmod(i, width)
        step = 1 if group % 2 == pairing else -1
        moves.append((i, (group + step) % groups * width + place))
    return lax.ppermute(array, axis, moves)


def shift(array, axis, step):
    devices = lax.axis_size(axis)
    return lax.ppermute(array, axis, [(i, (i + step) % devices) for i in range(devices)])


def shards(pore_mask, phase_labels, velocity):
    own_x, own_y = pore_mask.shape[0], pore_mask.shape[1]
    slab = lax.axis_index("slab")
    core, chip = slab % 2, slab // 2 % 2
    colour = jnp.where(pore_mask > 0, 2.0 * phase_labels.astype(jnp.float32) - 1.0, 0.0)
    block = jnp.concatenate([colour[None], velocity])
    before = shift(block[:, :, own_y - HALO :], "cross", 1)
    after = shift(block[:, :, :HALO], "cross", -1)
    own = jnp.concatenate([before, block, after], axis=2)
    inner = exchange(own, "slab", 2, 0)
    outer = exchange(own, "slab", 2, 1)
    passed = jnp.where(core == chip, inner, outer)
    partner = exchange(jnp.concatenate([own, passed], axis=1), "slab", 1, 0)
    inner_at = jnp.where(chip == 0, HALO + 2 * own_x, 0)
    partner_at = jnp.where(core == 0, HALO + own_x, HALO - own_x)
    places = jnp.stack([inner_at, HALO + 2 * own_x - inner_at, partner_at, 2 * HALO - partner_at])
    return advance(places.astype(jnp.int32), own, inner, outer, partner)


def solution(mesh):
    in_specs = (P("slab", "cross", None), P("slab", "cross", None), P(None, "slab", "cross", None))
    out_specs = (P("slab", "cross", None), P(None, "slab", "cross", None))
    return jax.shard_map(shards, mesh=mesh, in_specs=in_specs, out_specs=out_specs, check_vma=False)
```

```python
import jax
import jax.numpy as jnp
from jax import lax
from jax.experimental import pallas as pl
from jax.experimental.pallas import tpu as pltpu
from jax.sharding import PartitionSpec as P


STEPS = 4
HALO = 2 * STEPS
PAD = 8

lattice_dirs = [
    (0, 0, 0),
    (1, 0, 0),
    (-1, 0, 0),
    (0, 1, 0),
    (0, -1, 0),
    (0, 0, 1),
    (0, 0, -1),
    (1, 1, 0),
    (-1, -1, 0),
    (1, -1, 0),
    (-1, 1, 0),
    (1, 0, 1),
    (-1, 0, -1),
    (1, 0, -1),
    (-1, 0, 1),
    (0, 1, 1),
    (0, -1, -1),
    (0, 1, -1),
    (0, -1, 1),
]
relax_red = 1.0
relax_blue = 0.7
tension = 0.1
segregation = 0.7
driving = 0.001
LANES = 128
SEALED = -3.0e38


def turn(value, amount):
    return pltpu.roll(value, amount % LANES, axis=1)


def gradient_of(tint, x, y):
    at = {(dx, dy): tint[x + dx, pl.ds(y + dy, 8), :] for dx in (-1, 0, 1) for dy in (-1, 0, 1)}
    along_x = {dy: at[1, dy] - at[-1, dy] for dy in (-1, 0, 1)}
    along_y = {dx: at[dx, 1] - at[dx, -1] for dx in (-1, 0, 1)}
    gx = (along_x[0] + along_x[0]) + (along_x[1] + along_x[-1]) + (turn(along_x[0], 1) + turn(along_x[0], -1))
    gy = (along_y[0] + along_y[0]) + (along_y[1] + along_y[-1]) + (turn(along_y[0], 1) + turn(along_y[0], -1))
    mixed = (at[0, 0] + at[0, 0]) + (at[1, 0] + at[-1, 0]) + (at[0, 1] + at[0, -1])
    gz = turn(mixed, -1) - turn(mixed, 1)
    return (gx, gy, gz), at[0, 0]


def collide_tile(pulled, density, flow, omega, mass, colour, gradient):
    _, uy, uz = flow
    gx, gy, gz = gradient
    grad_sq = gx * gx + gy * gy + gz * gz
    part = tension / 36.0 / 144.0
    tensed = [part * g for g in gradient]
    if pulled is None:
        drift = [(3.0 / 36.0) * u for u in flow]
        curve = [(4.5 / 36.0) * u for u in flow]
        push = 3.0 * driving / 36.0
        level = jnp.where(colour != 0.0, 1.0 / 36.0, jnp.nan)
    else:
        level = omega * density * (1.0 / 36.0)
        triple = 3.0 * level
        drift = [triple * u for u in flow]
        curve = [1.5 * d for d in drift]
        push = (3.0 * driving / 36.0) * density
    square = [c * u + t * g for c, u, t, g in zip(curve, flow, tensed, gradient)]
    total = square[0] + square[1] + square[2]
    tense_sq = (2.0 * part) * grad_sq
    even = level - (1.0 / 3.0) * (total + tense_sq)
    drift = [drift[0] + push, drift[1], drift[2]]
    twice_c = [curve[0] + curve[0], curve[1] + curve[1]]
    twice_t = [tensed[0] + tensed[0], tensed[1] + tensed[1]]
    cross = {
        (0, 1): twice_c[0] * uy + twice_t[0] * gy,
        (0, 2): twice_c[0] * uz + twice_t[0] * gz,
        (1, 2): twice_c[1] * uz + twice_t[1] * gz,
    }
    base = [even + s for s in square]
    rest = 12.0 * (even + tense_sq)
    post = [None] * 19
    keep = None if pulled is None else 1.0 - omega

    def put(member, symmetric, skew):
        if pulled is None:
            post[member] = symmetric + skew
            post[member + 1] = symmetric - skew
        else:
            post[member] = keep * pulled[member] + (symmetric + skew)
            post[member + 1] = keep * pulled[member + 1] + (symmetric - skew)

    post[0] = rest if pulled is None else keep * pulled[0] + rest
    for axis in range(3):
        put(1 + 2 * axis, base[axis] + base[axis], drift[axis] + drift[axis])
    for a, b, first, second in ((0, 1, 7, 9), (0, 2, 11, 13), (1, 2, 15, 17)):
        plane = base[a] + square[b]
        put(first, plane + cross[a, b], drift[a] + drift[b])
        put(second, plane - cross[a, b], drift[a] - drift[b])

    shrink = jnp.minimum(lax.rsqrt(grad_sq), 2.0 / 12.0)
    if mass is None:
        eighth = jnp.where(colour != 0.0, 0.125, jnp.nan)
        sway = [0.5 * u for u in flow]
    else:
        eighth = 0.125 * mass
        half = 0.5 * mass
        sway = [half * u for u in flow]
    tinted = eighth * colour
    sharpen = (0.5 * segregation) * (eighth - tinted * colour) * shrink
    fluxes = []
    for axis in range(3):
        slope = sway[axis] * colour + sharpen * gradient[axis]
        fluxes += [eighth + sway[axis], eighth - sway[axis], tinted + slope, tinted - slope]
    return post, fluxes


def kernel(par_ref, e_ref, a_ref, b_ref, s_ref, phase_ref, out_ref, vel, flux, star, held, fluid, *doubled):
    tints, amounts = doubled[0:2], doubled[2:4]
    own_x, own_y = phase_ref.shape[0], phase_ref.shape[1]
    rows, cols = own_x + 2 * HALO, own_y + 2 * HALO
    for ref, origin, start in (
        (e_ref, 0, HALO),
        (a_ref, 0, par_ref[0]),
        (b_ref, 0, par_ref[1]),
        (s_ref, 0, par_ref[2]),
        (s_ref, own_x, par_ref[3]),
    ):
        for r in range(own_x):
            for y in range(0, cols, 8):
                tints[0][start + r, pl.ds(PAD + y, 8), :] = ref[0, origin + r, pl.ds(y, 8), :]
                for c in range(3):
                    vel[c, start + r, pl.ds(y, 8), :] = ref[1 + c, origin + r, pl.ds(y, 8), :]

    def spread(low, high, groups, body, tiles=None):
        count = len(groups)
        height = max(1, (tiles or count) // count)

        def some(i, carry):
            for x in range(height):
                for y in groups:
                    body(low + i * height + x, y)
            return carry

        lax.fori_loop(0, (high - low) // height, some, 0)

    def pull(ref, lead, member, x, y):
        cx, cy, cz = lattice_dirs[member]
        value = ref[lead, x - cx, pl.ds(PAD + y - cy, 8), :]
        return turn(value, cz) if cz else value

    def write(x, y, post, fluxes):
        for member in range(19):
            star[member, x, pl.ds(PAD + y, 8), :] = post[member]
        for k in range(12):
            flux[k, x, pl.ds(PAD + y, 8), :] = fluxes[k]

    def first(x, y):
        gradient, colour = gradient_of(tints[0], x, PAD + y)
        flow = [vel[c, x, pl.ds(y, 8), :] for c in range(3)]
        post, fluxes = collide_tile(None, None, flow, None, None, colour, gradient)
        write(x, y, post, fluxes)
        amounts[0][x, pl.ds(PAD + y, 8), :] = jnp.ones_like(colour)

    whole, inner = range(0, cols, 8), range(4, cols - 4, 8)
    spread(1, rows - 1, whole, first)

    def streamed(source, x, y):
        amount = 0.25 * amounts[source][x, pl.ds(PAD + y, 8), :]
        tinted = amount * tints[source][x, pl.ds(PAD + y, 8), :]
        values = [star[0, x, pl.ds(PAD + y, 8), :]]
        for member in range(1, 19):
            other = member + 1 if member % 2 == 1 else member - 1
            moved = pull(star, member, member, x, y)
            free = moved > SEALED
            values.append(jnp.where(free, moved, star[other, x, pl.ds(PAD + y, 8), :]))
            if member < 7:
                axis, sign = divmod(member - 1, 2)
                here, back = 4 * axis + sign, 4 * axis + 1 - sign
                amount = amount + jnp.where(
                    free, pull(flux, here, member, x, y), flux[back, x, pl.ds(PAD + y, 8), :]
                )
                tinted = tinted + jnp.where(
                    free, pull(flux, here + 2, member, x, y), flux[back + 2, x, pl.ds(PAD + y, 8), :]
                )
        pore = values[0] > SEALED
        return amount, jnp.where(pore, tinted / amount, 0.0), pore, values

    for step in range(2, STEPS + 1):
        source = step % 2

        def arrive(x, y, source=source):
            amount, colour, _, values = streamed(source, x, y)
            amounts[1 - source][x, pl.ds(PAD + y, 8), :] = amount
            tints[1 - source][x, pl.ds(PAD + y, 8), :] = colour
            for member in range(19):
                held[member, x, pl.ds(PAD + y, 8), :] = values[member]
            summed = {m: values[m] + values[m + 1] for m in range(1, 19, 2)}
            gap = {m: values[m] - values[m + 1] for m in range(1, 19, 2)}
            density = values[0] + (
                ((summed[1] + summed[3]) + (summed[5] + summed[7]))
                + ((summed[9] + summed[11]) + (summed[13] + summed[15]))
                + summed[17]
            )
            jx = gap[1] + ((gap[7] + gap[9]) + (gap[11] + gap[13]))
            jy = gap[3] + ((gap[7] - gap[9]) + (gap[15] + gap[17]))
            jz = gap[5] + ((gap[11] - gap[13]) + (gap[15] - gap[17]))
            lighten = 1.0 / density
            for k, value in enumerate((jx * lighten, jy * lighten, jz * lighten, density)):
                fluid[k, x, pl.ds(PAD + y, 8), :] = value

        def later(x, y, source=source):
            gradient, colour = gradient_of(tints[1 - source], x, PAD + y)
            held_here = [held[member, x, pl.ds(PAD + y, 8), :] for member in range(19)]
            flow = [fluid[k, x, pl.ds(PAD + y, 8), :] for k in range(3)]
            density = fluid[3, x, pl.ds(PAD + y, 8), :]
            omega = 1.0 / (0.5 * (relax_red + relax_blue) + (0.5 * (relax_red - relax_blue)) * colour)
            amount = amounts[1 - source][x, pl.ds(PAD + y, 8), :]
            post, fluxes = collide_tile(held_here, density, flow, omega, amount, colour, gradient)
            write(x, y, post, fluxes)

        groups = whole if step == 2 else inner
        spread(2 * step - 2, rows - 2 * step + 2, groups, arrive, 4 * len(groups))
        spread(2 * step - 1, rows - 2 * step + 1, groups, later, 2 * len(groups))

    def final(x, y):
        _, colour, pore, values = streamed((STEPS + 1) % 2, x, y)
        phase_ref[x - HALO, pl.ds(y - HALO, 8), :] = colour
        flow = [vel[c, x, pl.ds(y, 8), :] for c in range(3)]
        speed = flow[0] * flow[0] + flow[1] * flow[1] + flow[2] * flow[2]
        for member in range(19):
            weight = 1.0 / 3.0 if member == 0 else 1.0 / 18.0 if member < 7 else 1.0 / 36.0
            dot = sum(float(c) * u for c, u in zip(lattice_dirs[member], flow) if c != 0)
            start = weight * (1.0 + 3.0 * dot + 4.5 * dot * dot - 1.5 * speed)
            out_ref[member, x - HALO, pl.ds(y - HALO, 8), :] = jnp.where(pore, values[member], start)

    spread(HALO, HALO + own_x, range(HALO, HALO + own_y, 8), final)


def advance(places, own, inner, outer, partner):
    own_x, cols = own.shape[1], own.shape[2]
    own_y = cols - 2 * HALO
    rows = own_x + 2 * HALO
    wide = cols + 2 * PAD
    vmem = pl.BlockSpec(memory_space=pltpu.VMEM)
    return pl.pallas_call(
        kernel,
        out_shape=(
            jax.ShapeDtypeStruct((own_x, own_y, LANES), jnp.float32),
            jax.ShapeDtypeStruct((19, own_x, own_y, LANES), jnp.float32),
        ),
        in_specs=[pl.BlockSpec(memory_space=pltpu.SMEM)] + [vmem] * 4,
        out_specs=(vmem, vmem),
        scratch_shapes=[
            pltpu.VMEM((3, rows, cols, LANES), jnp.float32),
            pltpu.VMEM((12, rows, wide, LANES), jnp.float32),
            pltpu.VMEM((19, rows, wide, LANES), jnp.float32),
            pltpu.VMEM((19, rows, wide, LANES), jnp.float32),
            pltpu.VMEM((4, rows, wide, LANES), jnp.float32),
        ]
        + [pltpu.VMEM((rows, wide, LANES), jnp.float32)] * 4,
        compiler_params=pltpu.CompilerParams(vmem_limit_bytes=48 * 1024 * 1024),
    )(places, own, inner, outer, partner)


def exchange(array, axis, width, pairing):
    devices = lax.axis_size(axis)
    groups = devices // width
    moves = []
    for i in range(devices):
        group, place = divmod(i, width)
        step = 1 if group % 2 == pairing else -1
        moves.append((i, (group + step) % groups * width + place))
    return lax.ppermute(array, axis, moves)


def shift(array, axis, step):
    devices = lax.axis_size(axis)
    return lax.ppermute(array, axis, [(i, (i + step) % devices) for i in range(devices)])


def shards(pore_mask, phase_labels, velocity):
    own_x, own_y = pore_mask.shape[0], pore_mask.shape[1]
    slab = lax.axis_index("slab")
    core, chip = slab % 2, slab // 2 % 2
    colour = jnp.where(pore_mask > 0, 2.0 * phase_labels.astype(jnp.float32) - 1.0, 0.0)
    block = jnp.concatenate([colour[None], velocity])
    before = shift(block[:, :, own_y - HALO :], "cross", 1)
    after = shift(block[:, :, :HALO], "cross", -1)
    own = jnp.concatenate([before, block, after], axis=2)
    inner = exchange(own, "slab", 2, 0)
    outer = exchange(own, "slab", 2, 1)
    passed = jnp.where(core == chip, inner, outer)
    partner = exchange(jnp.concatenate([own, passed], axis=1), "slab", 1, 0)
    inner_at = jnp.where(chip == 0, HALO + 2 * own_x, 0)
    partner_at = jnp.where(core == 0, HALO + own_x, HALO - own_x)
    places = jnp.stack([inner_at, HALO + 2 * own_x - inner_at, partner_at, 2 * HALO - partner_at])
    return advance(places.astype(jnp.int32), own, inner, outer, partner)


def solution(mesh):
    in_specs = (P("slab", "cross", None), P("slab", "cross", None), P(None, "slab", "cross", None))
    out_specs = (P("slab", "cross", None), P(None, "slab", "cross", None))
    return jax.shard_map(shards, mesh=mesh, in_specs=in_specs, out_specs=out_specs, check_vma=False)
```

```python
import jax
import jax.numpy as jnp
from jax import lax
from jax.experimental import pallas as pl
from jax.experimental.pallas import tpu as pltpu
from jax.sharding import PartitionSpec as P


STEPS = 4
HALO = 2 * STEPS
PAD = 8

lattice_dirs = [
    (0, 0, 0),
    (1, 0, 0),
    (-1, 0, 0),
    (0, 1, 0),
    (0, -1, 0),
    (0, 0, 1),
    (0, 0, -1),
    (1, 1, 0),
    (-1, -1, 0),
    (1, -1, 0),
    (-1, 1, 0),
    (1, 0, 1),
    (-1, 0, -1),
    (1, 0, -1),
    (-1, 0, 1),
    (0, 1, 1),
    (0, -1, -1),
    (0, 1, -1),
    (0, -1, 1),
]
relax_red = 1.0
relax_blue = 0.7
tension = 0.1
segregation = 0.7
driving = 0.001
LANES = 128
SEALED = -3.0e38


def turn(value, amount):
    return pltpu.roll(value, amount % LANES, axis=1)


def gradient_of(tint, x, y):
    at = {(dx, dy): tint[x + dx, pl.ds(y + dy, 8), :] for dx in (-1, 0, 1) for dy in (-1, 0, 1)}
    along_x = {dy: at[1, dy] - at[-1, dy] for dy in (-1, 0, 1)}
    along_y = {dx: at[dx, 1] - at[dx, -1] for dx in (-1, 0, 1)}
    gx = (along_x[0] + along_x[0]) + (along_x[1] + along_x[-1]) + (turn(along_x[0], 1) + turn(along_x[0], -1))
    gy = (along_y[0] + along_y[0]) + (along_y[1] + along_y[-1]) + (turn(along_y[0], 1) + turn(along_y[0], -1))
    mixed = (at[0, 0] + at[0, 0]) + (at[1, 0] + at[-1, 0]) + (at[0, 1] + at[0, -1])
    gz = turn(mixed, -1) - turn(mixed, 1)
    return (gx, gy, gz), at[0, 0]


def collide_tile(pulled, density, flow, omega, mass, colour, gradient):
    _, uy, uz = flow
    gx, gy, gz = gradient
    grad_sq = gx * gx + gy * gy + gz * gz
    part = tension / 36.0 / 144.0
    tensed = [part * g for g in gradient]
    if pulled is None:
        drift = [(3.0 / 36.0) * u for u in flow]
        curve = [(4.5 / 36.0) * u for u in flow]
        push = 3.0 * driving / 36.0
        level = jnp.where(colour != 0.0, 1.0 / 36.0, jnp.nan)
    else:
        level = omega * density * (1.0 / 36.0)
        triple = 3.0 * level
        drift = [triple * u for u in flow]
        curve = [1.5 * d for d in drift]
        push = (3.0 * driving / 36.0) * density
    square = [c * u + t * g for c, u, t, g in zip(curve, flow, tensed, gradient)]
    total = square[0] + square[1] + square[2]
    tense_sq = (2.0 * part) * grad_sq
    even = level - (1.0 / 3.0) * (total + tense_sq)
    drift = [drift[0] + push, drift[1], drift[2]]
    twice_c = [curve[0] + curve[0], curve[1] + curve[1]]
    twice_t = [tensed[0] + tensed[0], tensed[1] + tensed[1]]
    cross = {
        (0, 1): twice_c[0] * uy + twice_t[0] * gy,
        (0, 2): twice_c[0] * uz + twice_t[0] * gz,
        (1, 2): twice_c[1] * uz + twice_t[1] * gz,
    }
    base = [even + s for s in square]
    rest = 12.0 * (even + tense_sq)
    post = [None] * 19
    keep = None if pulled is None else 1.0 - omega

    def put(member, symmetric, skew):
        if pulled is None:
            post[member] = symmetric + skew
            post[member + 1] = symmetric - skew
        else:
            post[member] = keep * pulled[member] + (symmetric + skew)
            post[member + 1] = keep * pulled[member + 1] + (symmetric - skew)

    post[0] = rest if pulled is None else keep * pulled[0] + rest
    for axis in range(3):
        put(1 + 2 * axis, base[axis] + base[axis], drift[axis] + drift[axis])
    for a, b, first, second in ((0, 1, 7, 9), (0, 2, 11, 13), (1, 2, 15, 17)):
        plane = base[a] + square[b]
        put(first, plane + cross[a, b], drift[a] + drift[b])
        put(second, plane - cross[a, b], drift[a] - drift[b])

    shrink = jnp.minimum(lax.rsqrt(grad_sq), 2.0 / 12.0)
    if mass is None:
        eighth = jnp.where(colour != 0.0, 0.125, jnp.nan)
        sway = [0.5 * u for u in flow]
    else:
        eighth = 0.125 * mass
        half = 0.5 * mass
        sway = [half * u for u in flow]
    tinted = eighth * colour
    sharpen = (0.5 * segregation) * (eighth - tinted * colour) * shrink
    fluxes = []
    for axis in range(3):
        slope = sway[axis] * colour + sharpen * gradient[axis]
        fluxes += [eighth + sway[axis], eighth - sway[axis], tinted + slope, tinted - slope]
    return post, fluxes


def gather(ref, start, vel, tint):
    for r in range(ref.shape[1]):
        for y in range(0, ref.shape[2], 8):
            tint[start + r, pl.ds(PAD + y, 8), :] = ref[0, r, pl.ds(y, 8), :]
            for c in range(3):
                vel[c, start + r, pl.ds(y, 8), :] = ref[1 + c, r, pl.ds(y, 8), :]


def write(star, flux, x, y, post, fluxes):
    for member in range(19):
        star[member, x, pl.ds(PAD + y, 8), :] = post[member]
    for k in range(12):
        flux[k, x, pl.ds(PAD + y, 8), :] = fluxes[k]


def first_row(x, vel, tint, flux, star):
    for y in range(0, vel.shape[2], 8):
        gradient, colour = gradient_of(tint, x, PAD + y)
        flow = [vel[c, x, pl.ds(y, 8), :] for c in range(3)]
        write(star, flux, x, y, *collide_tile(None, None, flow, None, None, colour, gradient))


def early_kernel(par_ref, own_ref, inner_ref, partner_ref, vel, tint, flux, star):
    own_x = own_ref.shape[1]
    gather(own_ref, HALO, vel, tint)
    gather(inner_ref, par_ref[0], vel, tint)
    gather(partner_ref, par_ref[2], vel, tint)
    near, side = jnp.minimum(par_ref[2], HALO) + 1, par_ref[0] + 1
    long = 2 * own_x - 2

    def row(i, carry):
        first_row(jnp.where(i < long, near + i, side + i - long), vel, tint, flux, star)
        return carry

    lax.fori_loop(0, long + own_x - 2, row, 0)


def kernel(par_ref, outer_ref, passed_ref, _vel, _tint, _flux, _star, phase_ref, out_ref, vel, tint, flux, star, held, fluid, *doubled):
    tints, amounts = (tint, doubled[0]), doubled[1:3]
    own_x, own_y = phase_ref.shape[0], phase_ref.shape[1]
    rows, cols = own_x + 2 * HALO, own_y + 2 * HALO
    gather(outer_ref, par_ref[1], vel, tint)
    gather(passed_ref, par_ref[3], vel, tint)

    def spread(low, high, groups, body, tiles=None):
        count = len(groups)
        height = max(1, (tiles or count) // count)

        def some(i, carry):
            for x in range(height):
                for y in groups:
                    body(low + i * height + x, y)
            return carry

        lax.fori_loop(0, (high - low) // height, some, 0)

    def pull(ref, lead, member, x, y):
        cx, cy, cz = lattice_dirs[member]
        value = ref[lead, x - cx, pl.ds(PAD + y - cy, 8), :]
        return turn(value, cz) if cz else value

    near, side = jnp.minimum(par_ref[2], HALO) + 1, par_ref[0] + 1
    long, short = 2 * own_x - 2, own_x - 2
    low, high = jnp.minimum(near, side), jnp.maximum(near, side)
    low_skip = jnp.where(near < side, long, short)

    def row(i, carry):
        x = 1 + i
        x = x + jnp.where(x >= low, low_skip, 0)
        x = x + jnp.where(x >= high, long + short - low_skip, 0)
        first_row(x, vel, tint, flux, star)
        return carry

    lax.fori_loop(0, rows - 2 - long - short, row, 0)

    whole, inner = range(0, cols, 8), range(4, cols - 4, 8)

    def streamed(source, x, y):
        amount = 0.25 if source is None else 0.25 * amounts[source][x, pl.ds(PAD + y, 8), :]
        source = source or 0
        tinted = amount * tints[source][x, pl.ds(PAD + y, 8), :]
        values = [star[0, x, pl.ds(PAD + y, 8), :]]
        for member in range(1, 19):
            other = member + 1 if member % 2 == 1 else member - 1
            moved = pull(star, member, member, x, y)
            free = moved > SEALED
            values.append(jnp.where(free, moved, star[other, x, pl.ds(PAD + y, 8), :]))
            if member < 7:
                axis, sign = divmod(member - 1, 2)
                here, back = 4 * axis + sign, 4 * axis + 1 - sign
                amount = amount + jnp.where(
                    free, pull(flux, here, member, x, y), flux[back, x, pl.ds(PAD + y, 8), :]
                )
                tinted = tinted + jnp.where(
                    free, pull(flux, here + 2, member, x, y), flux[back + 2, x, pl.ds(PAD + y, 8), :]
                )
        pore = values[0] > SEALED
        return amount, jnp.where(pore, tinted / amount, 0.0), pore, values

    for step in range(2, STEPS + 1):
        source = step % 2

        def arrive(x, y, source=source, before=None if step == 2 else source):
            amount, colour, _, values = streamed(before, x, y)
            amounts[1 - source][x, pl.ds(PAD + y, 8), :] = amount
            tints[1 - source][x, pl.ds(PAD + y, 8), :] = colour
            for member in range(19):
                held[member, x, pl.ds(PAD + y, 8), :] = values[member]
            summed = {m: values[m] + values[m + 1] for m in range(1, 19, 2)}
            gap = {m: values[m] - values[m + 1] for m in range(1, 19, 2)}
            density = values[0] + (
                ((summed[1] + summed[3]) + (summed[5] + summed[7]))
                + ((summed[9] + summed[11]) + (summed[13] + summed[15]))
                + summed[17]
            )
            jx = gap[1] + ((gap[7] + gap[9]) + (gap[11] + gap[13]))
            jy = gap[3] + ((gap[7] - gap[9]) + (gap[15] + gap[17]))
            jz = gap[5] + ((gap[11] - gap[13]) + (gap[15] - gap[17]))
            lighten = 1.0 / density
            for k, value in enumerate((jx * lighten, jy * lighten, jz * lighten, density)):
                fluid[k, x, pl.ds(PAD + y, 8), :] = value

        def later(x, y, source=source):
            gradient, colour = gradient_of(tints[1 - source], x, PAD + y)
            held_here = [held[member, x, pl.ds(PAD + y, 8), :] for member in range(19)]
            flow = [fluid[k, x, pl.ds(PAD + y, 8), :] for k in range(3)]
            density = fluid[3, x, pl.ds(PAD + y, 8), :]
            omega = 1.0 / (0.5 * (relax_red + relax_blue) + (0.5 * (relax_red - relax_blue)) * colour)
            amount = amounts[1 - source][x, pl.ds(PAD + y, 8), :]
            post, fluxes = collide_tile(held_here, density, flow, omega, amount, colour, gradient)
            write(star, flux, x, y, post, fluxes)

        groups = whole if step == 2 else inner
        spread(2 * step - 2, rows - 2 * step + 2, groups, arrive, 4 * len(groups))
        spread(2 * step - 1, rows - 2 * step + 1, groups, later, 2 * len(groups))

    def final(x, y):
        _, colour, pore, values = streamed((STEPS + 1) % 2, x, y)
        phase_ref[x - HALO, pl.ds(y - HALO, 8), :] = colour
        flow = [vel[c, x, pl.ds(y, 8), :] for c in range(3)]
        speed = flow[0] * flow[0] + flow[1] * flow[1] + flow[2] * flow[2]
        for member in range(19):
            weight = 1.0 / 3.0 if member == 0 else 1.0 / 18.0 if member < 7 else 1.0 / 36.0
            dot = sum(float(c) * u for c, u in zip(lattice_dirs[member], flow) if c != 0)
            start = weight * (1.0 + 3.0 * dot + 4.5 * dot * dot - 1.5 * speed)
            out_ref[member, x - HALO, pl.ds(y - HALO, 8), :] = jnp.where(pore, values[member], start)

    spread(HALO, HALO + own_x, range(HALO, HALO + own_y, 8), final)


def advance(places, own, inner, outer, partner, passed):
    own_x, cols = own.shape[1], own.shape[2]
    own_y = cols - 2 * HALO
    rows, wide = own_x + 2 * HALO, cols + 2 * PAD
    vmem, smem = pl.BlockSpec(memory_space=pltpu.VMEM), pl.BlockSpec(memory_space=pltpu.SMEM)

    def shape(*dims):
        return jax.ShapeDtypeStruct((*dims, LANES), jnp.float32)

    state_shapes = (shape(3, rows, cols), shape(rows, wide), shape(12, rows, wide), shape(19, rows, wide))
    state = pl.pallas_call(
        early_kernel,
        out_shape=state_shapes,
        in_specs=[smem] + [vmem] * 3,
        out_specs=(vmem,) * 4,
        compiler_params=pltpu.CompilerParams(vmem_limit_bytes=2 * 1024 * 1024),
    )(places, own, inner, partner)
    return pl.pallas_call(
        kernel,
        out_shape=(shape(own_x, own_y), shape(19, own_x, own_y)) + state_shapes,
        in_specs=[smem] + [vmem] * 6,
        out_specs=(vmem,) * 6,
        scratch_shapes=[
            pltpu.VMEM((19, rows, wide, LANES), jnp.float32),
            pltpu.VMEM((4, rows, wide, LANES), jnp.float32),
        ]
        + [pltpu.VMEM((rows, wide, LANES), jnp.float32)] * 3,
        input_output_aliases={3: 2, 4: 3, 5: 4, 6: 5},
        compiler_params=pltpu.CompilerParams(vmem_limit_bytes=16 * 1024 * 1024),
    )(places, outer, passed, *state)[:2]


def exchange(array, axis, width, pairing):
    devices = lax.axis_size(axis)
    groups = devices // width
    moves = []
    for i in range(devices):
        group, place = divmod(i, width)
        step = 1 if group % 2 == pairing else -1
        moves.append((i, (group + step) % groups * width + place))
    return lax.ppermute(array, axis, moves)


def shift(array, axis, step):
    devices = lax.axis_size(axis)
    return lax.ppermute(array, axis, [(i, (i + step) % devices) for i in range(devices)])


def shards(pore_mask, phase_labels, velocity):
    own_x, own_y = pore_mask.shape[0], pore_mask.shape[1]
    slab = lax.axis_index("slab")
    core, chip = slab % 2, slab // 2 % 2
    colour = jnp.where(pore_mask > 0, 2.0 * phase_labels.astype(jnp.float32) - 1.0, 0.0)
    block = lax.optimization_barrier(jnp.concatenate([colour[None], velocity]))
    before = shift(block[:, :, own_y - HALO :], "cross", 1)
    after = shift(block[:, :, :HALO], "cross", -1)
    own = jnp.concatenate([before, block, after], axis=2)
    inner = exchange(own, "slab", 2, 0)
    outer = exchange(own, "slab", 2, 1)
    partner = exchange(own, "slab", 1, 0)
    passed = exchange(jnp.where(core == chip, inner, outer), "slab", 1, 0)
    inner_at = jnp.where(chip == 0, HALO + 2 * own_x, 0)
    partner_at = jnp.where(core == 0, HALO + own_x, HALO - own_x)
    places = jnp.stack([inner_at, HALO + 2 * own_x - inner_at, partner_at, 2 * HALO - partner_at])
    return advance(places.astype(jnp.int32), own, inner, outer, partner, passed)


def solution(mesh):
    in_specs = (P("slab", "cross", None), P("slab", "cross", None), P(None, "slab", "cross", None))
    out_specs = (P("slab", "cross", None), P(None, "slab", "cross", None))
    return jax.shard_map(shards, mesh=mesh, in_specs=in_specs, out_specs=out_specs, check_vma=False)
```

```python
import jax
import jax.numpy as jnp
from jax import lax
from jax.experimental import pallas as pl
from jax.experimental.pallas import tpu as pltpu
from jax.sharding import PartitionSpec as P


STEPS = 4
HALO = 2 * STEPS
PAD = 8

lattice_dirs = [
    (0, 0, 0),
    (1, 0, 0),
    (-1, 0, 0),
    (0, 1, 0),
    (0, -1, 0),
    (0, 0, 1),
    (0, 0, -1),
    (1, 1, 0),
    (-1, -1, 0),
    (1, -1, 0),
    (-1, 1, 0),
    (1, 0, 1),
    (-1, 0, -1),
    (1, 0, -1),
    (-1, 0, 1),
    (0, 1, 1),
    (0, -1, -1),
    (0, 1, -1),
    (0, -1, 1),
]
relax_red = 1.0
relax_blue = 0.7
tension = 0.1
segregation = 0.7
driving = 0.001
LANES = 128
SEALED = -3.0e38


def turn(value, amount):
    return pltpu.roll(value, amount % LANES, axis=1)


def gradient_of(tint, x, y):
    at = {(dx, dy): tint[x + dx, pl.ds(y + dy, 8), :] for dx in (-1, 0, 1) for dy in (-1, 0, 1)}
    along_x = {dy: at[1, dy] - at[-1, dy] for dy in (-1, 0, 1)}
    along_y = {dx: at[dx, 1] - at[dx, -1] for dx in (-1, 0, 1)}
    gx = (along_x[0] + along_x[0]) + (along_x[1] + along_x[-1]) + (turn(along_x[0], 1) + turn(along_x[0], -1))
    gy = (along_y[0] + along_y[0]) + (along_y[1] + along_y[-1]) + (turn(along_y[0], 1) + turn(along_y[0], -1))
    mixed = (at[0, 0] + at[0, 0]) + (at[1, 0] + at[-1, 0]) + (at[0, 1] + at[0, -1])
    gz = turn(mixed, -1) - turn(mixed, 1)
    return (gx, gy, gz), at[0, 0]


def collide_tile(pulled, density, flow, omega, mass, colour, gradient):
    _, uy, uz = flow
    gx, gy, gz = gradient
    grad_sq = gx * gx + gy * gy + gz * gz
    part = tension / 36.0 / 144.0
    tensed = [part * g for g in gradient]
    if pulled is None:
        drift = [(3.0 / 36.0) * u for u in flow]
        curve = [(4.5 / 36.0) * u for u in flow]
        push = 3.0 * driving / 36.0
        level = jnp.where(colour != 0.0, 1.0 / 36.0, jnp.nan)
    else:
        level = omega * density * (1.0 / 36.0)
        triple = 3.0 * level
        drift = [triple * u for u in flow]
        curve = [1.5 * d for d in drift]
        push = (3.0 * driving / 36.0) * density
    square = [c * u + t * g for c, u, t, g in zip(curve, flow, tensed, gradient)]
    total = square[0] + square[1] + square[2]
    tense_sq = (2.0 * part) * grad_sq
    even = level - (1.0 / 3.0) * (total + tense_sq)
    drift = [drift[0] + push, drift[1], drift[2]]
    twice_c = [curve[0] + curve[0], curve[1] + curve[1]]
    twice_t = [tensed[0] + tensed[0], tensed[1] + tensed[1]]
    cross = {
        (0, 1): twice_c[0] * uy + twice_t[0] * gy,
        (0, 2): twice_c[0] * uz + twice_t[0] * gz,
        (1, 2): twice_c[1] * uz + twice_t[1] * gz,
    }
    base = [even + s for s in square]
    rest = 12.0 * (even + tense_sq)
    post = [None] * 19
    keep = None if pulled is None else 1.0 - omega

    def put(member, symmetric, skew):
        if pulled is None:
            post[member] = symmetric + skew
            post[member + 1] = symmetric - skew
        else:
            post[member] = keep * pulled[member] + (symmetric + skew)
            post[member + 1] = keep * pulled[member + 1] + (symmetric - skew)

    post[0] = rest if pulled is None else keep * pulled[0] + rest
    for axis in range(3):
        put(1 + 2 * axis, base[axis] + base[axis], drift[axis] + drift[axis])
    for a, b, first, second in ((0, 1, 7, 9), (0, 2, 11, 13), (1, 2, 15, 17)):
        plane = base[a] + square[b]
        put(first, plane + cross[a, b], drift[a] + drift[b])
        put(second, plane - cross[a, b], drift[a] - drift[b])

    shrink = jnp.minimum(lax.rsqrt(grad_sq), 2.0 / 12.0)
    if mass is None:
        eighth = jnp.where(colour != 0.0, 0.125, jnp.nan)
        sway = [0.5 * u for u in flow]
    else:
        eighth = 0.125 * mass
        half = 0.5 * mass
        sway = [half * u for u in flow]
    tinted = eighth * colour
    sharpen = (0.5 * segregation) * (eighth - tinted * colour) * shrink
    fluxes = []
    for axis in range(3):
        slope = sway[axis] * colour + sharpen * gradient[axis]
        fluxes += [eighth + sway[axis], eighth - sway[axis], tinted + slope, tinted - slope]
    return post, fluxes


def gather(ref, start, vel, tint):
    for r in range(ref.shape[1]):
        for y in range(0, ref.shape[2], 8):
            tint[start + r, pl.ds(PAD + y, 8), :] = ref[0, r, pl.ds(y, 8), :]
            for c in range(3):
                vel[c, start + r, pl.ds(y, 8), :] = ref[1 + c, r, pl.ds(y, 8), :]


def write(star, flux, x, y, post, fluxes):
    for member in range(19):
        star[member, x, pl.ds(PAD + y, 8), :] = post[member]
    for k in range(12):
        flux[k, x, pl.ds(PAD + y, 8), :] = fluxes[k]


def first_row(x, vel, tint, flux, star):
    for y in range(0, vel.shape[2], 8):
        gradient, colour = gradient_of(tint, x, PAD + y)
        flow = [vel[c, x, pl.ds(y, 8), :] for c in range(3)]
        write(star, flux, x, y, *collide_tile(None, None, flow, None, None, colour, gradient))


def early_kernel(par_ref, own_ref, inner_ref, partner_ref, vel, tint, flux, star):
    own_x = own_ref.shape[1]
    gather(own_ref, HALO, vel, tint)
    gather(inner_ref, par_ref[0], vel, tint)
    gather(partner_ref, par_ref[2], vel, tint)
    near, side = jnp.minimum(par_ref[2], HALO) + 1, par_ref[0] + 1
    long = 2 * own_x - 2

    def row(i, carry):
        first_row(jnp.where(i < long, near + i, side + i - long), vel, tint, flux, star)
        return carry

    lax.fori_loop(0, long + own_x - 2, row, 0)


def middle_kernel(par_ref, outer_ref, _vel, _tint, _flux, _star, vel, tint, flux, star):
    own_x = outer_ref.shape[1]
    gather(outer_ref, par_ref[1], vel, tint)
    joint = jnp.where(par_ref[2] > HALO, par_ref[2] + own_x, par_ref[2]) - 1
    short = own_x - 2

    def row(i, carry):
        first_row(jnp.where(i < short, par_ref[1] + 1 + i, joint + i - short), vel, tint, flux, star)
        return carry

    lax.fori_loop(0, short + 2, row, 0)


def kernel(par_ref, passed_ref, _vel, _tint, _flux, _star, phase_ref, out_ref, vel, tint, flux, star, held, fluid, *doubled):
    tints, amounts = (tint, doubled[0]), doubled[1:3]
    own_x, own_y = phase_ref.shape[0], phase_ref.shape[1]
    rows, cols = own_x + 2 * HALO, own_y + 2 * HALO
    gather(passed_ref, par_ref[3], vel, tint)

    def spread(low, high, groups, body, tiles=None):
        count = len(groups)
        height = max(1, (tiles or count) // count)

        def some(i, carry):
            for x in range(height):
                for y in groups:
                    body(low + i * height + x, y)
            return carry

        lax.fori_loop(0, (high - low) // height, some, 0)

    def pull(ref, lead, member, x, y):
        cx, cy, cz = lattice_dirs[member]
        value = ref[lead, x - cx, pl.ds(PAD + y - cy, 8), :]
        return turn(value, cz) if cz else value

    def row(i, carry):
        first_row(par_ref[3] - 1 + i, vel, tint, flux, star)
        return carry

    lax.fori_loop(0, own_x + 2, row, 0)

    whole, inner = range(0, cols, 8), range(4, cols - 4, 8)

    def streamed(source, x, y):
        amount = 0.25 if source is None else 0.25 * amounts[source][x, pl.ds(PAD + y, 8), :]
        source = source or 0
        tinted = amount * tints[source][x, pl.ds(PAD + y, 8), :]
        values = [star[0, x, pl.ds(PAD + y, 8), :]]
        for member in range(1, 19):
            other = member + 1 if member % 2 == 1 else member - 1
            moved = pull(star, member, member, x, y)
            free = moved > SEALED
            values.append(jnp.where(free, moved, star[other, x, pl.ds(PAD + y, 8), :]))
            if member < 7:
                axis, sign = divmod(member - 1, 2)
                here, back = 4 * axis + sign, 4 * axis + 1 - sign
                amount = amount + jnp.where(
                    free, pull(flux, here, member, x, y), flux[back, x, pl.ds(PAD + y, 8), :]
                )
                tinted = tinted + jnp.where(
                    free, pull(flux, here + 2, member, x, y), flux[back + 2, x, pl.ds(PAD + y, 8), :]
                )
        pore = values[0] > SEALED
        return amount, jnp.where(pore, tinted / amount, 0.0), pore, values

    for step in range(2, STEPS + 1):
        source = step % 2

        def arrive(x, y, source=source, before=None if step == 2 else source):
            amount, colour, _, values = streamed(before, x, y)
            amounts[1 - source][x, pl.ds(PAD + y, 8), :] = amount
            tints[1 - source][x, pl.ds(PAD + y, 8), :] = colour
            for member in range(19):
                held[member, x, pl.ds(PAD + y, 8), :] = values[member]
            summed = {m: values[m] + values[m + 1] for m in range(1, 19, 2)}
            gap = {m: values[m] - values[m + 1] for m in range(1, 19, 2)}
            density = values[0] + (
                ((summed[1] + summed[3]) + (summed[5] + summed[7]))
                + ((summed[9] + summed[11]) + (summed[13] + summed[15]))
                + summed[17]
            )
            jx = gap[1] + ((gap[7] + gap[9]) + (gap[11] + gap[13]))
            jy = gap[3] + ((gap[7] - gap[9]) + (gap[15] + gap[17]))
            jz = gap[5] + ((gap[11] - gap[13]) + (gap[15] - gap[17]))
            lighten = 1.0 / density
            for k, value in enumerate((jx * lighten, jy * lighten, jz * lighten, density)):
                fluid[k, x, pl.ds(PAD + y, 8), :] = value

        def later(x, y, source=source):
            gradient, colour = gradient_of(tints[1 - source], x, PAD + y)
            held_here = [held[member, x, pl.ds(PAD + y, 8), :] for member in range(19)]
            flow = [fluid[k, x, pl.ds(PAD + y, 8), :] for k in range(3)]
            density = fluid[3, x, pl.ds(PAD + y, 8), :]
            omega = 1.0 / (0.5 * (relax_red + relax_blue) + (0.5 * (relax_red - relax_blue)) * colour)
            amount = amounts[1 - source][x, pl.ds(PAD + y, 8), :]
            post, fluxes = collide_tile(held_here, density, flow, omega, amount, colour, gradient)
            write(star, flux, x, y, post, fluxes)

        groups = whole if step == 2 else inner
        spread(2 * step - 2, rows - 2 * step + 2, groups, arrive, (rows - 4 * step + 4) // 2 * len(groups))
        spread(2 * step - 1, rows - 2 * step + 1, groups, later, 2 * len(groups))

    def final(x, y):
        _, colour, pore, values = streamed((STEPS + 1) % 2, x, y)
        phase_ref[x - HALO, pl.ds(y - HALO, 8), :] = colour
        flow = [vel[c, x, pl.ds(y, 8), :] for c in range(3)]
        speed = flow[0] * flow[0] + flow[1] * flow[1] + flow[2] * flow[2]
        for member in range(19):
            weight = 1.0 / 3.0 if member == 0 else 1.0 / 18.0 if member < 7 else 1.0 / 36.0
            dot = sum(float(c) * u for c, u in zip(lattice_dirs[member], flow) if c != 0)
            start = weight * (1.0 + 3.0 * dot + 4.5 * dot * dot - 1.5 * speed)
            out_ref[member, x - HALO, pl.ds(y - HALO, 8), :] = jnp.where(pore, values[member], start)

    spread(HALO, HALO + own_x, range(HALO, HALO + own_y, 8), final)


def advance(places, own, inner, outer, partner, passed):
    own_x, cols = own.shape[1], own.shape[2]
    own_y = cols - 2 * HALO
    rows, wide = own_x + 2 * HALO, cols + 2 * PAD
    vmem, smem = pl.BlockSpec(memory_space=pltpu.VMEM), pl.BlockSpec(memory_space=pltpu.SMEM)

    def shape(*dims):
        return jax.ShapeDtypeStruct((*dims, LANES), jnp.float32)

    state_shapes = (shape(3, rows, cols), shape(rows, wide), shape(12, rows, wide), shape(19, rows, wide))
    state = pl.pallas_call(
        early_kernel,
        out_shape=state_shapes,
        in_specs=[smem] + [vmem] * 3,
        out_specs=(vmem,) * 4,
        compiler_params=pltpu.CompilerParams(vmem_limit_bytes=2 * 1024 * 1024),
    )(places, own, inner, partner)
    state = pl.pallas_call(
        middle_kernel,
        out_shape=state_shapes,
        in_specs=[smem] + [vmem] * 5,
        out_specs=(vmem,) * 4,
        input_output_aliases={2: 0, 3: 1, 4: 2, 5: 3},
        compiler_params=pltpu.CompilerParams(vmem_limit_bytes=2 * 1024 * 1024),
    )(places, outer, *state)
    return pl.pallas_call(
        kernel,
        out_shape=(shape(own_x, own_y), shape(19, own_x, own_y)) + state_shapes,
        in_specs=[smem] + [vmem] * 5,
        out_specs=(vmem,) * 6,
        scratch_shapes=[
            pltpu.VMEM((19, rows, wide, LANES), jnp.float32),
            pltpu.VMEM((4, rows, wide, LANES), jnp.float32),
        ]
        + [pltpu.VMEM((rows, wide, LANES), jnp.float32)] * 3,
        input_output_aliases={2: 2, 3: 3, 4: 4, 5: 5},
        compiler_params=pltpu.CompilerParams(vmem_limit_bytes=16 * 1024 * 1024),
    )(places, passed, *state)[:2]


def exchange(array, axis, width, pairing):
    devices = lax.axis_size(axis)
    groups = devices // width
    moves = []
    for i in range(devices):
        group, place = divmod(i, width)
        step = 1 if group % 2 == pairing else -1
        moves.append((i, (group + step) % groups * width + place))
    return lax.ppermute(array, axis, moves)


def shift(array, axis, step):
    devices = lax.axis_size(axis)
    return lax.ppermute(array, axis, [(i, (i + step) % devices) for i in range(devices)])


def shards(pore_mask, phase_labels, velocity):
    own_x, own_y = pore_mask.shape[0], pore_mask.shape[1]
    slab = lax.axis_index("slab")
    core, chip = slab % 2, slab // 2 % 2
    colour = jnp.where(pore_mask > 0, 2.0 * phase_labels.astype(jnp.float32) - 1.0, 0.0)
    block = lax.optimization_barrier(jnp.concatenate([colour[None], velocity]))
    before = shift(block[:, :, own_y - HALO :], "cross", 1)
    after = shift(block[:, :, :HALO], "cross", -1)
    own = jnp.concatenate([before, block, after], axis=2)
    inner = exchange(own, "slab", 2, 0)
    outer = exchange(own, "slab", 2, 1)
    partner = exchange(own, "slab", 1, 0)
    passed = exchange(jnp.where(core == chip, inner, outer), "slab", 1, 0)
    inner_at = jnp.where(chip == 0, HALO + 2 * own_x, 0)
    partner_at = jnp.where(core == 0, HALO + own_x, HALO - own_x)
    places = jnp.stack([inner_at, HALO + 2 * own_x - inner_at, partner_at, 2 * HALO - partner_at])
    return advance(places.astype(jnp.int32), own, inner, outer, partner, passed)


def solution(mesh):
    in_specs = (P("slab", "cross", None), P("slab", "cross", None), P(None, "slab", "cross", None))
    out_specs = (P("slab", "cross", None), P(None, "slab", "cross", None))
    return jax.shard_map(shards, mesh=mesh, in_specs=in_specs, out_specs=out_specs, check_vma=False)
```
